32 devices in a mesh: dp: 16 (over z, y, x), ctx: 2 (over core).
Axes of the slice: x: 2, y: 2, z: 4, core: 2. Of those that a mesh axis runs over, the one named last changes fastest.
Arguments:
- inputs: bfloat16 [16, 4, 16, 16, 128], P('dp', 'ctx'), may hold values from -90 to 90
- cotangent: bfloat16 [16, 4, 16, 16, 128], P('dp', 'ctx'), may hold values from -18 to 18
- conv_weight: bfloat16 [3, 3, 3, 128, 128], replicated, may hold values from -0.109375 to 0.109375
- norm_gain: float32 [128], replicated, may hold values from 0.1 to 1.9
- norm_bias: float32 [128], replicated, may hold values from -3 to 3
Outputs:
- input_grad: bfloat16 [16, 4, 16, 16, 128], P('dp', 'ctx')
- weight_grad: float32 [3, 3, 3, 128, 128], replicated
- gain_grad: float32 [128], replicated
- bias_grad: float32 [128], replicated
The draws below stay inside these ranges and needn't reach their ends.
All inputs are finite; a program needn't handle non-finite values.
Results may differ from the reference program's by a relative error of at most 0.0027.
Values may be sent and summed in bfloat16 or wider, within the bound.
A program may use at most 64 MiB of HBM per device.

```python
import math
import jax
import jax.numpy as jnp
from jax import lax

C = 128
GROUPS = 32
SIDE = 16
CLIPS = 16
FRAMES = 4
CELLS = 16384


def frame_rise(key_frames):
    position = jnp.arange(FRAMES, dtype=jnp.float32) / (FRAMES - 1)
    rough = jnp.exp(jax.random.uniform(key_frames, (CLIPS, FRAMES), jnp.float32, -0.35, 0.35))
    return (3.0 ** position)[None, :] * rough


def draw_inputs(key, part):
    keys = jax.random.split(jax.random.fold_in(key, 11), 4)
    shape_all = (CLIPS, FRAMES, SIDE, SIDE, C)
    rising = frame_rise(keys[0])
    channel_scale = jnp.exp(jax.random.uniform(keys[1], (C,), jnp.float32, math.log(0.4), math.log(4.0)))
    offset = jax.random.uniform(keys[2], (C,), jnp.float32, -1.0, 1.0)
    noise = jnp.clip(jax.random.normal(keys[3], shape_all, jnp.float32), -4.0, 4.0)
    values = offset + rising[:, :, None, None, None] * channel_scale * noise
    return values.astype(jnp.bfloat16)


def draw_cotangent(key, part):
    keys = jax.random.split(jax.random.fold_in(key, 23), 3)
    shape_all = (CLIPS, FRAMES, SIDE, SIDE, C)
    rising = frame_rise(keys[0])
    noise = jnp.clip(jax.random.normal(keys[2], shape_all, jnp.float32), -4.0, 4.0)
    values = rising[:, :, None, None, None] * noise
    return values.astype(jnp.bfloat16)


def normal_values(own_key, extent, deviation, bound, kind=jnp.bfloat16):
    drawn = deviation * jax.random.normal(own_key, extent, jnp.float32)
    return jnp.clip(drawn, min=-bound, max=bound).astype(kind)


def setup_inputs(seed: int = 0) -> dict:
    key_list = jax.random.split(jax.random.key(seed), 6)
    return {
        "inputs": draw_inputs(jax.random.fold_in(key_list[5], 71), 0),
        "cotangent": draw_cotangent(jax.random.fold_in(key_list[5], 71), 0),
        "conv_weight": normal_values(key_list[2], (3, 3, 3, C, C), (27 * C) ** -0.5, 0.109375),
        "norm_gain": jnp.clip(1.0 + 0.18 * jax.random.normal(key_list[3], (C,), jnp.float32), 0.1, 1.9),
        "norm_bias": normal_values(key_list[4], (C,), 0.5, 3.0, jnp.float32),
    }


epsilon = 1e-06

def group_average(per_channel, members):
    grouped = per_channel.reshape(GROUPS, -1).sum(axis=1, keepdims=True) / members
    return jnp.broadcast_to(grouped, (GROUPS, per_channel.shape[0] // GROUPS)).reshape(-1)

def kernel_terms(padded_act, grad_flat, frames_n, side_len, channels):
    pieces = []
    for tap_time in range(3):
        for tap_row in range(3):
            columns = jnp.concatenate([padded_act[tap_time:tap_time + frames_n, tap_row:tap_row + side_len, tap_col:tap_col + side_len] for tap_col in range(3)], axis=-1).reshape(-1, 3 * channels)
            pieces.append(lax.dot_general(columns, grad_flat, (((0,), (0,)), ((), ())), preferred_element_type=jnp.float32))
    return jnp.stack(pieces).reshape(3, 3, 3, channels, channels)

def spread_back(grad_ext, weight_turned, frames_out, side_len, channels):
    total_grad = jnp.zeros((frames_out * side_len * side_len, channels), jnp.float32)
    for tap_time in range(3):
        for tap_row in range(3):
            columns = jnp.concatenate([grad_ext[2 - tap_time:2 - tap_time + frames_out, 2 - tap_row:2 - tap_row + side_len, 2 - tap_col:2 - tap_col + side_len] for tap_col in range(3)], axis=-1).reshape(-1, 3 * channels)
            total_grad = total_grad + jnp.dot(columns, weight_turned[tap_time, tap_row].reshape(3 * channels, channels), preferred_element_type=jnp.float32)
    return total_grad.reshape(frames_out, side_len, side_len, channels)

def clip_backward(clip_inputs, clip_grad, conv_weight, norm_gain, norm_bias):
    frames_n, side_len, channels = (clip_inputs.shape[0], clip_inputs.shape[1], clip_inputs.shape[3])
    values = clip_inputs.astype(jnp.float32)
    flat_values = values.reshape(-1, channels)
    members = flat_values.shape[0] * (channels // GROUPS)
    average = group_average(flat_values.sum(axis=0), members)
    centered = flat_values - average
    spread = group_average((centered * centered).sum(axis=0), members)
    inverse_std = lax.rsqrt(spread + epsilon)
    normed = (values - average) * inverse_std
    shifted = normed * norm_gain + norm_bias
    activation = jax.nn.silu(shifted).astype(jnp.bfloat16)
    padded_act = jnp.concatenate([activation[:1], activation[:1], activation], axis=0)
    padded_act = jnp.pad(padded_act, ((0, 0), (1, 1), (1, 1), (0, 0)))
    grad_flat = clip_grad.reshape(-1, channels)
    kernel_sum = kernel_terms(padded_act, grad_flat, frames_n, side_len, channels)
    blank = jnp.zeros((2, side_len, side_len, channels), jnp.bfloat16)
    grad_ext = jnp.concatenate([blank, clip_grad, blank], axis=0)
    grad_ext = jnp.pad(grad_ext, ((0, 0), (1, 1), (1, 1), (0, 0)))
    weight_turned = jnp.transpose(conv_weight, (0, 1, 2, 4, 3))
    pad_grad = spread_back(grad_ext, weight_turned, frames_n + 2, side_len, channels)
    act_grad = pad_grad[2:].at[0].add(pad_grad[0] + pad_grad[1])
    sigmoid_val = jax.nn.sigmoid(shifted)
    pre_grad = act_grad * sigmoid_val * (1.0 + shifted * (1.0 - sigmoid_val))
    normed_grad = pre_grad * norm_gain
    first_mean = group_average(normed_grad.reshape(-1, channels).sum(axis=0), members)
    second_mean = group_average((normed_grad * normed).reshape(-1, channels).sum(axis=0), members)
    input_grad = (inverse_std * (normed_grad - first_mean - normed * second_mean)).astype(jnp.bfloat16)
    gain_part = (pre_grad * normed).reshape(-1, channels).sum(axis=0)
    bias_part = pre_grad.reshape(-1, channels).sum(axis=0)
    return (input_grad, kernel_sum, gain_part, bias_part)

def reference(inputs, cotangent, conv_weight, norm_gain, norm_bias):
    channels = inputs.shape[4]

    def step_clip(carry, pair):
        result = clip_backward(pair[0], pair[1], conv_weight, norm_gain, norm_bias)
        return ((carry[0] + result[1], carry[1] + result[2], carry[2] + result[3]), result[0])
    start = (jnp.zeros((3, 3, 3, channels, channels), jnp.float32), jnp.zeros((channels,), jnp.float32), jnp.zeros((channels,), jnp.float32))
    totals, input_grad = lax.scan(step_clip, start, (inputs, cotangent))
    scale_val = 1.0 / jnp.sqrt(jnp.float32(CELLS))
    return (input_grad, totals[0] * scale_val, totals[1] * scale_val, totals[2] * scale_val)
```

```python
import functools
import jax
import jax.numpy as jnp
from jax import lax
from jax.experimental import pallas as pl
from jax.experimental.pallas import tpu as pltpu
from jax.sharding import PartitionSpec as P

GROUPS = 32


epsilon = 1e-06


def from_behind(x, axis, by):
    count = lax.axis_size(axis)
    pairs = [(i, i + by) for i in range(count) if 0 <= i + by < count]
    return lax.ppermute(x, axis, pairs)


def group_average(per_channel, members):
    grouped = per_channel.reshape(GROUPS, -1).sum(axis=1, keepdims=True) / members
    return jnp.broadcast_to(grouped, (GROUPS, per_channel.shape[0] // GROUPS)).reshape(-1)


def kernel_terms(padded_act, grad_flat, frames_n, side_len, channels):
    pieces = []
    for tap_time in range(3):
        for tap_row in range(3):
            columns = jnp.concatenate(
                [
                    padded_act[
                        tap_time : tap_time + frames_n,
                        tap_row : tap_row + side_len,
                        tap_col : tap_col + side_len,
                    ]
                    for tap_col in range(3)
                ],
                axis=-1,
            ).reshape(-1, 3 * channels)
            pieces.append(
                lax.dot_general(
                    columns, grad_flat, (((0,), (0,)), ((), ())), preferred_element_type=jnp.float32
                )
            )
    return pieces


def spread_back(grad_ext, weight_turned, frames_out, side_len, channels):
    total_grad = jnp.zeros((frames_out * side_len * side_len, channels), jnp.float32)
    for tap_time in range(3):
        for tap_row in range(3):
            columns = jnp.concatenate(
                [
                    grad_ext[
                        2 - tap_time : 2 - tap_time + frames_out,
                        2 - tap_row : 2 - tap_row + side_len,
                        2 - tap_col : 2 - tap_col + side_len,
                    ]
                    for tap_col in range(3)
                ],
                axis=-1,
            ).reshape(-1, 3 * channels)
            total_grad = total_grad + jnp.dot(
                columns,
                weight_turned[tap_time, tap_row].reshape(3 * channels, channels),
                preferred_element_type=jnp.float32,
            )
    return total_grad.reshape(frames_out, side_len, side_len, channels)


def plane_back(plane, weight_plane, side_len, channels):
    padded = jnp.pad(plane, ((1, 1), (1, 1), (0, 0)))
    total_grad = jnp.zeros((side_len * side_len, channels), jnp.float32)
    for tap_row in range(3):
        columns = jnp.concatenate(
            [
                padded[2 - tap_row : 2 - tap_row + side_len, 2 - tap_col : 2 - tap_col + side_len]
                for tap_col in range(3)
            ],
            axis=-1,
        ).reshape(-1, 3 * channels)
        total_grad = total_grad + jnp.dot(
            columns,
            weight_plane[tap_row].reshape(3 * channels, channels),
            preferred_element_type=jnp.float32,
        )
    return total_grad.reshape(side_len, side_len, channels)


def step_list(dp_count, ctx_count):
    steps = []
    for axis, count in (("ctx", ctx_count), ("dp", dp_count)):
        bit = 1
        while bit < count:
            steps.append((axis, bit))
            bit *= 2
    return steps


def narrow(step):
    return step in (1, 2)


def sum_kernel(steps, rows, kern_ref, small_ref, out_ref, small_out, acc, gath, *rest):
    count = len(steps)
    recvs = rest[:count]
    sends = dict(zip([i for i in range(count) if narrow(i)], rest[count:]))
    small_send, small_recv, sems_s, sems_r, small_s, small_r, back_s, back_r = rest[-8:]
    partners = [{axis: lax.axis_index(axis) ^ bit} for axis, bit in steps]
    barrier = pltpu.get_barrier_semaphore()
    for partner in partners:
        pl.semaphore_signal(
            barrier, inc=1, device_id=partner, device_id_type=pl.DeviceIdType.MESH
        )
    pl.semaphore_wait(barrier, count)

    def remote(src, dst, send_sem, recv_sem, partner):
        return pltpu.make_async_remote_copy(
            src_ref=src,
            dst_ref=dst,
            send_sem=send_sem,
            recv_sem=recv_sem,
            device_id=partner,
            device_id_type=pl.DeviceIdType.MESH,
        )

    start = jnp.int32(0)
    length = rows
    small_now = small_ref[...]
    starts = []
    for i, (axis, bit) in enumerate(steps):
        starts.append((start, length))
        half = length // 2
        mine = (lax.axis_index(axis) // bit) % 2
        keep = pl.multiple_of(start + mine * half, 16)
        away = pl.multiple_of(start + (1 - mine) * half, 16)
        held = kern_ref if i == 0 else acc
        if narrow(i):
            sends[i][...] = held[pl.ds(away, half), :].astype(jnp.bfloat16)
            source = sends[i]
        else:
            source = held.at[pl.ds(away, half), :]
        small_send[i] = small_now
        copy = remote(source, recvs[i], sems_s.at[i], sems_r.at[i], partners[i])
        copy.start()
        small_copy = remote(
            small_send.at[i], small_recv.at[i], small_s.at[i], small_r.at[i], partners[i]
        )
        small_copy.start()
        copy.wait()
        acc[pl.ds(keep, half), :] = held[pl.ds(keep, half), :] + recvs[i][...].astype(jnp.float32)
        small_copy.wait()
        small_now = small_now + small_recv[i]
        start = keep
        length = half
    small_out[...] = small_now
    gath[pl.ds(start, length), :] = acc[pl.ds(start, length), :].astype(jnp.bfloat16)
    for i in reversed(range(count)):
        piece = gath.at[pl.ds(start, length), :]
        copy = remote(piece, piece, back_s.at[i], back_r.at[i], partners[i])
        copy.start()
        copy.wait()
        start, length = starts[i]
        start = pl.multiple_of(start, 16)
    out_ref[...] = gath[...]


def sum_everywhere(pieces, small, channels):
    steps = step_list(lax.axis_size("dp"), lax.axis_size("ctx"))
    count = len(steps)
    devices = 2**count
    used = sum(piece.shape[0] for piece in pieces)
    unit = 16 * devices
    rows = -(-used // unit) * unit
    blank = jnp.zeros((rows - used, channels), jnp.float32)
    stacked = jnp.concatenate(list(pieces) + [blank], axis=0)
    recvs = [
        pltpu.VMEM((rows >> (i + 1), channels), jnp.bfloat16 if narrow(i) else jnp.float32)
        for i in range(count)
    ]
    sends = [
        pltpu.VMEM((rows >> (i + 1), channels), jnp.bfloat16) for i in range(count) if narrow(i)
    ]
    vmem = pl.BlockSpec(memory_space=pltpu.VMEM)
    total, small_total = pl.pallas_call(
        functools.partial(sum_kernel, steps, rows),
        out_shape=(
            jax.ShapeDtypeStruct((rows, channels), jnp.bfloat16),
            jax.ShapeDtypeStruct(small.shape, jnp.float32),
        ),
        in_specs=[vmem, vmem],
        out_specs=(vmem, vmem),
        scratch_shapes=[
            pltpu.VMEM((rows, channels), jnp.float32),
            pltpu.VMEM((rows, channels), jnp.bfloat16),
            *recvs,
            *sends,
            pltpu.VMEM((count,) + small.shape, jnp.float32),
            pltpu.VMEM((count,) + small.shape, jnp.float32),
            *[pltpu.SemaphoreType.DMA((count,)) for _ in range(6)],
        ],
        compiler_params=pltpu.CompilerParams(
            collective_id=0, has_side_effects=True, vmem_limit_bytes=48 * 1024 * 1024
        ),
    )(stacked, small)
    return total[:used], small_total


def body(inputs, cotangent, conv_weight, norm_gain, norm_bias):
    frames_n, side_len, channels = (inputs.shape[1], inputs.shape[2], inputs.shape[4])
    ctx_count = lax.axis_size("ctx")
    leading = lax.axis_index("ctx") == 0
    members = frames_n * side_len * side_len * ctx_count * (channels // GROUPS)
    values = inputs[0].astype(jnp.float32)
    flat_values = values.reshape(-1, channels)
    totals, squares = lax.psum(
        (flat_values.sum(axis=0), (flat_values * flat_values).sum(axis=0)), "ctx"
    )
    average = group_average(totals, members)
    spread = group_average(squares, members) - average * average
    inverse_std = lax.rsqrt(spread + epsilon)
    normed_val = (values - average) * inverse_std
    shifted_val = normed_val * norm_gain + norm_bias
    activation = jax.nn.silu(shifted_val).astype(jnp.bfloat16)
    prior = from_behind(activation, "ctx", 1)
    prior = jnp.where(leading, jnp.broadcast_to(activation[:1], prior.shape), prior)
    padded_act = jnp.concatenate([prior, activation], axis=0)
    padded_act = jnp.pad(padded_act, ((0, 0), (1, 1), (1, 1), (0, 0)))
    grad_local = cotangent[0]
    after_frames = from_behind(grad_local, "ctx", -1)
    kernel_sum = kernel_terms(
        padded_act, grad_local.reshape(-1, channels), frames_n, side_len, channels
    )
    grad_ext = jnp.concatenate([grad_local, after_frames], axis=0)
    grad_ext = jnp.pad(grad_ext, ((0, 0), (1, 1), (1, 1), (0, 0)))
    weight_turned = jnp.transpose(conv_weight, (0, 1, 2, 4, 3))
    pad_grad = spread_back(grad_ext, weight_turned, frames_n, side_len, channels)

    def fold_terms():
        first_part = plane_back(grad_local[0], weight_turned[0], side_len, channels)
        second_part = plane_back(grad_local[1], weight_turned[0], side_len, channels)
        third_part = plane_back(grad_local[0], weight_turned[1], side_len, channels)
        return first_part + (second_part + third_part)

    def fold_empty():
        return jnp.zeros((side_len, side_len, channels), jnp.float32)

    folded = lax.cond(leading, fold_terms, fold_empty)
    act_grad = pad_grad.at[0].add(folded)
    sigmoid_val = jax.nn.sigmoid(shifted_val)
    pre_grad = act_grad * sigmoid_val * (1.0 + shifted_val * (1.0 - sigmoid_val))
    normed_grad = pre_grad * norm_gain
    first_total, second_total = lax.psum(
        (
            normed_grad.reshape(-1, channels).sum(axis=0),
            (normed_grad * normed_val).reshape(-1, channels).sum(axis=0),
        ),
        "ctx",
    )
    first_mean = group_average(first_total, members)
    second_mean = group_average(second_total, members)
    input_grad = (inverse_std * (normed_grad - first_mean - normed_val * second_mean)).astype(
        jnp.bfloat16
    )[None]
    gain_part = (pre_grad * normed_val).reshape(-1, channels).sum(axis=0)
    bias_part = pre_grad.reshape(-1, channels).sum(axis=0)
    small = jnp.concatenate(
        [gain_part[None], bias_part[None], jnp.zeros((6, channels), jnp.float32)], axis=0
    )
    kernel_all, small_all = sum_everywhere(kernel_sum, small, channels)
    kernel_all = kernel_all.astype(jnp.float32).reshape(3, 3, 3, channels, channels)
    gain_all, bias_all = small_all[0], small_all[1]
    cell_total = lax.axis_size("dp") * ctx_count * frames_n * side_len * side_len
    scale_val = 1.0 / jnp.sqrt(jnp.float32(cell_total))
    return (input_grad, kernel_all * scale_val, gain_all * scale_val, bias_all * scale_val)


def solution(mesh):
    placed = (P("dp", "ctx", None, None, None), P("dp", "ctx", None, None, None), P(), P(), P())
    return jax.shard_map(
        body,
        mesh=mesh,
        in_specs=placed,
        out_specs=(P("dp", "ctx", None, None, None), P(), P(), P()),
        check_vma=False,
    )
```

```python
import functools
import jax
import jax.numpy as jnp
from jax import lax
from jax.experimental import pallas as pl
from jax.experimental.pallas import tpu as pltpu
from jax.sharding import PartitionSpec as P

GROUPS = 32


epsilon = 1e-06


def from_behind(x, axis, by):
    count = lax.axis_size(axis)
    pairs = [(i, i + by) for i in range(count) if 0 <= i + by < count]
    return lax.ppermute(x, axis, pairs)


def group_average(per_channel, members):
    grouped = per_channel.reshape(GROUPS, -1).sum(axis=1, keepdims=True) / members
    return jnp.broadcast_to(grouped, (GROUPS, per_channel.shape[0] // GROUPS)).reshape(-1)


def kernel_terms(padded_act, grad_flat, frames_n, side_len, channels):
    pieces = []
    for tap_time in range(3):
        for tap_row in range(3):
            columns = jnp.concatenate(
                [
                    padded_act[
                        tap_time : tap_time + frames_n,
                        tap_row : tap_row + side_len,
                        tap_col : tap_col + side_len,
                    ]
                    for tap_col in range(3)
                ],
                axis=-1,
            ).reshape(-1, 3 * channels)
            pieces.append(
                lax.dot_general(
                    columns, grad_flat, (((0,), (0,)), ((), ())), preferred_element_type=jnp.float32
                )
            )
    return pieces


def spread_back(grad_ext, weight_turned, frames_out, side_len, channels):
    total_grad = jnp.zeros((frames_out * side_len * side_len, channels), jnp.float32)
    for tap_time in range(3):
        for tap_row in range(3):
            columns = jnp.concatenate(
                [
                    grad_ext[
                        2 - tap_time : 2 - tap_time + frames_out,
                        2 - tap_row : 2 - tap_row + side_len,
                        2 - tap_col : 2 - tap_col + side_len,
                    ]
                    for tap_col in range(3)
                ],
                axis=-1,
            ).reshape(-1, 3 * channels)
            total_grad = total_grad + jnp.dot(
                columns,
                weight_turned[tap_time, tap_row].reshape(3 * channels, channels),
                preferred_element_type=jnp.float32,
            )
    return total_grad.reshape(frames_out, side_len, side_len, channels)


def plane_back(plane, weight_plane, side_len, channels):
    padded = jnp.pad(plane, ((1, 1), (1, 1), (0, 0)))
    total_grad = jnp.zeros((side_len * side_len, channels), jnp.float32)
    for tap_row in range(3):
        columns = jnp.concatenate(
            [
                padded[2 - tap_row : 2 - tap_row + side_len, 2 - tap_col : 2 - tap_col + side_len]
                for tap_col in range(3)
            ],
            axis=-1,
        ).reshape(-1, 3 * channels)
        total_grad = total_grad + jnp.dot(
            columns,
            weight_plane[tap_row].reshape(3 * channels, channels),
            preferred_element_type=jnp.float32,
        )
    return total_grad.reshape(side_len, side_len, channels)


def step_list(dp_count, ctx_count, swapped):
    steps = []
    for axis, count in (("ctx", ctx_count), ("dp", dp_count)):
        bits = []
        bit = 1
        while bit < count:
            bits.append(bit)
            bit *= 2
        if swapped and axis == "dp":
            for i in range(0, len(bits) - 1, 2):
                bits[i], bits[i + 1] = bits[i + 1], bits[i]
        steps.extend((axis, bit) for bit in bits)
    return steps


def narrow(step):
    return step in (1, 2)


def sum_kernel(plans, kern_ref, small_ref, out_ref, small_out, acc, gath, *rest):
    count = len(plans[0][0])
    rest = list(rest)
    recvs = [[rest.pop(0) for _ in range(count)] for _ in plans]
    sends = [{i: rest.pop(0) for i in range(count) if narrow(i)} for _ in plans]
    small_send, small_recv, sems_s, sems_r, small_s, small_r, back_s, back_r = rest
    partners = [[{axis: lax.axis_index(axis) ^ bit} for axis, bit in plan[0]] for plan in plans]
    barrier = pltpu.get_barrier_semaphore()
    for partner in partners[0]:
        pl.semaphore_signal(
            barrier, inc=1, device_id=partner, device_id_type=pl.DeviceIdType.MESH
        )
    pl.semaphore_wait(barrier, count)

    def remote(src, dst, send_sem, recv_sem, partner):
        copy = pltpu.make_async_remote_copy(
            src_ref=src,
            dst_ref=dst,
            send_sem=send_sem,
            recv_sem=recv_sem,
            device_id=partner,
            device_id_type=pl.DeviceIdType.MESH,
        )
        copy.start()
        return copy

    def begin(p, i, start, length):
        axis, bit = plans[p][0][i]
        half = length // 2
        mine = (lax.axis_index(axis) // bit) % 2
        keep = pl.multiple_of(start + mine * half, 16)
        away = pl.multiple_of(start + (1 - mine) * half, 16)
        held = kern_ref if i == 0 else acc
        if narrow(i):
            sends[p][i][...] = held[pl.ds(away, half), :].astype(jnp.bfloat16)
            source = sends[p][i]
        else:
            source = held.at[pl.ds(away, half), :]
        copy = remote(source, recvs[p][i], sems_s.at[p, i], sems_r.at[p, i], partners[p][i])
        return copy, held, keep, half

    def begin_small(i, value):
        small_send[i] = value
        return remote(
            small_send.at[i], small_recv.at[i], small_s.at[i], small_r.at[i], partners[0][i]
        )

    spans = [[(plan[1], plan[2])] for plan in plans]
    flights = [begin(p, 0, plan[1], plan[2]) for p, plan in enumerate(plans)]
    small_now = small_ref[...]
    small_copy = begin_small(0, small_now)
    for i in range(count):
        for p in range(len(plans)):
            copy, held, keep, half = flights[p]
            copy.wait()
            acc[pl.ds(keep, half), :] = held[pl.ds(keep, half), :] + recvs[p][i][...].astype(
                jnp.float32
            )
            spans[p].append((keep, half))
            if i + 1 < count:
                flights[p] = begin(p, i + 1, keep, half)
        small_copy.wait()
        small_now = small_now + small_recv[i]
        if i + 1 < count:
            small_copy = begin_small(i + 1, small_now)
    small_out[...] = small_now

    def begin_back(p, i):
        start, length = spans[p][i + 1]
        piece = gath.at[pl.ds(start, length), :]
        return remote(piece, piece, back_s.at[p, i], back_r.at[p, i], partners[p][i])

    for p in range(len(plans)):
        start, length = spans[p][count]
        gath[pl.ds(start, length), :] = acc[pl.ds(start, length), :].astype(jnp.bfloat16)
        flights[p] = begin_back(p, count - 1)
    for i in reversed(range(count)):
        for p in range(len(plans)):
            flights[p].wait()
            if i > 0:
                flights[p] = begin_back(p, i - 1)
    out_ref[...] = gath[...]


def sum_everywhere(pieces, small, channels):
    dp_count, ctx_count = lax.axis_size("dp"), lax.axis_size("ctx")
    unit = 16 * dp_count * ctx_count
    used = sum(piece.shape[0] for piece in pieces)
    units = -(-used // unit)
    rows = units * unit
    first = (units + 1) // 2 * unit
    plans = [(step_list(dp_count, ctx_count, False), 0, first)]
    if first < rows:
        plans.append((step_list(dp_count, ctx_count, True), first, rows - first))
    count = len(plans[0][0])
    stacked = list(pieces)
    if rows > used:
        stacked.append(jnp.zeros((rows - used, channels), jnp.float32))
    stacked = jnp.concatenate(stacked, axis=0)
    recvs = [
        pltpu.VMEM((plan[2] >> (i + 1), channels), jnp.bfloat16 if narrow(i) else jnp.float32)
        for plan in plans
        for i in range(count)
    ]
    sends = [
        pltpu.VMEM((plan[2] >> (i + 1), channels), jnp.bfloat16)
        for plan in plans
        for i in range(count)
        if narrow(i)
    ]
    vmem = pl.BlockSpec(memory_space=pltpu.VMEM)
    many, one = (len(plans), count), (count,)
    total, small_total = pl.pallas_call(
        functools.partial(sum_kernel, plans),
        out_shape=(
            jax.ShapeDtypeStruct((rows, channels), jnp.bfloat16),
            jax.ShapeDtypeStruct(small.shape, jnp.float32),
        ),
        in_specs=[vmem, vmem],
        out_specs=(vmem, vmem),
        scratch_shapes=[
            pltpu.VMEM((rows, channels), jnp.float32),
            pltpu.VMEM((rows, channels), jnp.bfloat16),
            *recvs,
            *sends,
            pltpu.VMEM((count,) + small.shape, jnp.float32),
            pltpu.VMEM((count,) + small.shape, jnp.float32),
            *[pltpu.SemaphoreType.DMA(shape) for shape in (many, many, one, one, many, many)],
        ],
        compiler_params=pltpu.CompilerParams(
            collective_id=0, has_side_effects=True, vmem_limit_bytes=48 * 1024 * 1024
        ),
    )(stacked, small)
    return total[:used], small_total


def body(inputs, cotangent, conv_weight, norm_gain, norm_bias):
    frames_n, side_len, channels = (inputs.shape[1], inputs.shape[2], inputs.shape[4])
    ctx_count = lax.axis_size("ctx")
    leading = lax.axis_index("ctx") == 0
    members = frames_n * side_len * side_len * ctx_count * (channels // GROUPS)
    values = inputs[0].astype(jnp.float32)
    flat_values = values.reshape(-1, channels)
    totals, squares = lax.psum(
        (flat_values.sum(axis=0), (flat_values * flat_values).sum(axis=0)), "ctx"
    )
    average = group_average(totals, members)
    spread = group_average(squares, members) - average * average
    inverse_std = lax.rsqrt(spread + epsilon)
    normed_val = (values - average) * inverse_std
    shifted_val = normed_val * norm_gain + norm_bias
    activation = jax.nn.silu(shifted_val).astype(jnp.bfloat16)
    prior = from_behind(activation, "ctx", 1)
    prior = jnp.where(leading, jnp.broadcast_to(activation[:1], prior.shape), prior)
    padded_act = jnp.concatenate([prior, activation], axis=0)
    padded_act = jnp.pad(padded_act, ((0, 0), (1, 1), (1, 1), (0, 0)))
    grad_local = cotangent[0]
    after_frames = from_behind(grad_local, "ctx", -1)
    kernel_sum = kernel_terms(
        padded_act, grad_local.reshape(-1, channels), frames_n, side_len, channels
    )
    grad_ext = jnp.concatenate([grad_local, after_frames], axis=0)
    grad_ext = jnp.pad(grad_ext, ((0, 0), (1, 1), (1, 1), (0, 0)))
    weight_turned = jnp.transpose(conv_weight, (0, 1, 2, 4, 3))
    pad_grad = spread_back(grad_ext, weight_turned, frames_n, side_len, channels)

    def fold_terms():
        first_part = plane_back(grad_local[0], weight_turned[0], side_len, channels)
        second_part = plane_back(grad_local[1], weight_turned[0], side_len, channels)
        third_part = plane_back(grad_local[0], weight_turned[1], side_len, channels)
        return first_part + (second_part + third_part)

    def fold_empty():
        return jnp.zeros((side_len, side_len, channels), jnp.float32)

    folded = lax.cond(leading, fold_terms, fold_empty)
    act_grad = pad_grad.at[0].add(folded)
    sigmoid_val = jax.nn.sigmoid(shifted_val)
    pre_grad = act_grad * sigmoid_val * (1.0 + shifted_val * (1.0 - sigmoid_val))
    normed_grad = pre_grad * norm_gain
    first_total, second_total = lax.psum(
        (
            normed_grad.reshape(-1, channels).sum(axis=0),
            (normed_grad * normed_val).reshape(-1, channels).sum(axis=0),
        ),
        "ctx",
    )
    first_mean = group_average(first_total, members)
    second_mean = group_average(second_total, members)
    input_grad = (inverse_std * (normed_grad - first_mean - normed_val * second_mean)).astype(
        jnp.bfloat16
    )[None]
    gain_part = (pre_grad * normed_val).reshape(-1, channels).sum(axis=0)
    bias_part = pre_grad.reshape(-1, channels).sum(axis=0)
    small = jnp.concatenate(
        [gain_part[None], bias_part[None], jnp.zeros((6, channels), jnp.float32)], axis=0
    )
    kernel_all, small_all = sum_everywhere(kernel_sum, small, channels)
    kernel_all = kernel_all.astype(jnp.float32).reshape(3, 3, 3, channels, channels)
    gain_all, bias_all = small_all[0], small_all[1]
    cell_total = lax.axis_size("dp") * ctx_count * frames_n * side_len * side_len
    scale_val = 1.0 / jnp.sqrt(jnp.float32(cell_total))
    return (input_grad, kernel_all * scale_val, gain_all * scale_val, bias_all * scale_val)


def solution(mesh):
    placed = (P("dp", "ctx", None, None, None), P("dp", "ctx", None, None, None), P(), P(), P())
    return jax.shard_map(
        body,
        mesh=mesh,
        in_specs=placed,
        out_specs=(P("dp", "ctx", None, None, None), P(), P(), P()),
        check_vma=False,
    )
```
